32 devices in a mesh: clip: 2 (over x), tm: 2 (over core), space: 8 (over z, y).
Axes of the slice: x: 2, y: 2, z: 4, core: 2. Of those that a mesh axis runs over, the one named last changes fastest.
Arguments:
- queue_latents: float32 [16, 2, 16, 128], P(('clip', 'tm'), None, None, 'space'), parts along dimension 0, may hold values from -6 to 6
- fresh_noise: float32 [6, 2, 16, 128], P('clip', None, None, 'space'), parts along dimension 0, may hold values from -6 to 6
- slot_levels: int32 [16], P('clip'), parts along dimension 0, may hold values from 1 to 15, as said below
- level_table: float32 [16, 8, 1152], replicated, may hold values from -2.5 to 2.5
- embed_weight: float32 [16, 1152], replicated, may hold values from -1.5 to 1.5
- spatial_in: bfloat16 [1152, 1728], replicated, may hold values from -0.1875 to 0.1875
- spatial_out: bfloat16 [576, 1152], replicated, may hold values from -0.25 to 0.25
- temporal_in: bfloat16 [1152, 1728], replicated, may hold values from -0.1875 to 0.1875
- temporal_out: bfloat16 [576, 1152], replicated, may hold values from -0.25 to 0.25
- norm_gains: float32 [4, 72], replicated, may hold values from 0.1 to 1.9
- final_weight: float32 [1152, 16], replicated, may hold values from -0.1875 to 0.1875
Outputs:
- next_queue: float32 [16, 2, 16, 128], P(('clip', 'tm'), None, None, 'space'), parts along dimension 0
- denoised: float32 [16, 2, 16, 128], P(('clip', 'tm'), None, None, 'space'), parts along dimension 0
The draws below stay inside these ranges and needn't reach their ends.
There are 2 independent parts, one for each index of `clip`. The reference program is written for one: setup_inputs(seed, part) draws one part's arguments, and reference() takes and returns one part's arrays. A program takes and returns all parts, laid end to end along the dimension named above; an argument that names none is the same for every part. Nothing has to cross between parts.
Inputs may be any that keep to these rules, and one draw needn't show every extreme that they name: `slot_levels`: strictly rising along the queue; neighbouring slots differ by 1 or 2; the last slot holds 15.
All inputs are finite; a program needn't handle non-finite values.
Results may differ from the reference program's by a relative error of at most 0.0023.
Values may be sent and summed in bfloat16 or wider, within the bound.
A program may use at most 128 MiB of HBM per device.

```python
import math
import jax
import jax.numpy as jnp
from jax import lax

D = 1152
HEADS = 8
HD = 72
CH = 16
QUEUE = 8
FRAMES = 2
STEPS = 3
LEVELS = 16
SPACE_TOK = 128


def draw_slot_levels(key, part):
    gap_key = jax.random.fold_in(key, 11)
    gaps = jax.random.randint(gap_key, (QUEUE - 1,), 1, 3).astype(jnp.int32)
    above = jnp.cumsum(gaps[::-1])[::-1]
    top = jnp.full((1,), LEVELS - 1, jnp.int32)
    return jnp.concatenate([LEVELS - 1 - above, top]).astype(jnp.int32)


def steps_of(rng, extent, cuts, smallest, high):
    factor_of, own = 1.0, jax.random.fold_in(rng, 6)
    for position, blocks in cuts:
        draws = jnp.exp(jax.random.uniform(jax.random.fold_in(own, position), (blocks,), jnp.float32, smallest / len(cuts), high / len(cuts)))
        factor_of = factor_of * jnp.repeat(draws, extent[position] // blocks).reshape([-1 if axis == position else 1 for axis in range(len(extent))])
    return factor_of


def bell_draw(rng, dims, deviation, most, cuts=(), kind=jnp.bfloat16):
    values = jax.random.normal(rng, dims, jnp.float32) * deviation
    if len(cuts) > 0:
        values = steps_of(rng, dims, cuts, -0.22, 0.18) * values
    return jnp.clip(values, min=-most, max=most).astype(kind)


def setup_inputs(seed: int = 0, part: int = 0) -> dict:
    key_list = jax.random.split(jax.random.key(seed), 12)
    part_splits = jax.random.split(jax.random.fold_in(key_list[11], part), 12)
    queue_latents = bell_draw(part_splits[0], (QUEUE, FRAMES, CH, SPACE_TOK), 1.0, 6.0, ((0, 2), (3, 8)), jnp.float32)
    fresh_noise = bell_draw(part_splits[1], (STEPS, FRAMES, CH, SPACE_TOK), 1.0, 6.0, ((3, 8),), jnp.float32)
    slot_levels = draw_slot_levels(jax.random.fold_in(jax.random.fold_in(key_list[11], part), 71), part)
    level_table = bell_draw(key_list[3], (LEVELS, 8, D), 0.5, 2.5, (), jnp.float32)
    embed_weight = bell_draw(key_list[4], (CH, D), CH ** -0.5, 1.5, (), jnp.float32)
    spatial_in = bell_draw(key_list[5], (D, 3 * HEADS * HD), D ** -0.5, 0.1875)
    spatial_out = bell_draw(key_list[6], (HEADS * HD, D), (HEADS * HD) ** -0.5, 0.25)
    temporal_in = bell_draw(key_list[7], (D, 3 * HEADS * HD), D ** -0.5, 0.1875)
    temporal_out = bell_draw(key_list[8], (HEADS * HD, D), (HEADS * HD) ** -0.5, 0.25)
    norm_gains = jnp.clip(1.0 + 0.18 * jax.random.normal(key_list[9], (4, HD), jnp.float32), 0.1, 1.9)
    final_weight = bell_draw(key_list[10], (D, CH), D ** -0.5, 0.1875, (), jnp.float32)
    return dict(queue_latents=queue_latents, fresh_noise=fresh_noise, slot_levels=slot_levels, level_table=level_table, embed_weight=embed_weight, spatial_in=spatial_in, spatial_out=spatial_out, temporal_in=temporal_in, temporal_out=temporal_out, norm_gains=norm_gains, final_weight=final_weight)


epsilon = 1e-06
highest = lax.Precision.HIGHEST

def sincos(positions, width):
    half = width // 2
    rates = jnp.exp(-jnp.log(10000.0) * jnp.arange(half).astype(jnp.float32) / half)
    angles = positions.astype(jnp.float32)[:, None] * rates[None, :]
    return jnp.concatenate([jnp.sin(angles), jnp.cos(angles)], axis=-1)

def stored(values):
    return lax.optimization_barrier(values.astype(jnp.bfloat16))

def layer_norm(values):
    centered = values - lax.optimization_barrier(jnp.mean(values, axis=-1, keepdims=True))
    return centered * lax.rsqrt(lax.optimization_barrier(jnp.mean(centered * centered, axis=-1, keepdims=True)) + epsilon)

def modulate(hidden, table, shift_row, scale_row):
    shift = table[:, shift_row][:, None, None, :]
    scale = table[:, scale_row][:, None, None, :]
    return layer_norm(hidden) * (1.0 + scale) + shift

def head_norm(values, gain):
    values = values.astype(jnp.float32)
    scaled = values * lax.rsqrt(lax.optimization_barrier(jnp.mean(values * values, axis=-1, keepdims=True)) + epsilon)
    return stored(scaled * gain)

def project_heads(normed, weight, gains, first):
    projected = stored(jnp.dot(normed.reshape(-1, D), weight, preferred_element_type=jnp.float32))
    projected = projected.reshape(QUEUE * FRAMES, SPACE_TOK, 3, HEADS, HD)
    queries = head_norm(projected[:, :, 0], gains[first])
    keys = head_norm(projected[:, :, 1], gains[first + 1])
    return (queries, keys, projected[:, :, 2])

def spatial_frame(pieces):
    queries, keys, values = pieces
    scores = jnp.einsum('the,rhe->htr', queries.astype(jnp.float32), keys.astype(jnp.float32)) / math.sqrt(HD)
    weights = jnp.exp(scores)
    totals = lax.optimization_barrier(jnp.sum(weights, axis=-1))
    rounded = stored(weights).astype(jnp.float32)
    mixed = jnp.einsum('htr,rhe->the', rounded, values.astype(jnp.float32))
    return stored(mixed / jnp.transpose(totals)[:, :, None])

def temporal_mix(queries, keys, values):
    scores = jnp.einsum('fthe,gthe->thfg', queries.astype(jnp.float32), keys.astype(jnp.float32)) / math.sqrt(HD)
    weights = jnp.exp(scores)
    totals = jnp.transpose(lax.optimization_barrier(jnp.sum(weights, axis=-1)), (2, 0, 1))
    rounded = stored(weights).astype(jnp.float32)
    mixed = jnp.einsum('thfg,gthe->fthe', rounded, values.astype(jnp.float32))
    return stored(mixed / totals[..., None])

def denoise(latents, table, token_pos, frame_pos, embed_weight, spatial_in, spatial_out, temporal_in, temporal_out, norm_gains, final_weight):
    hidden = jnp.einsum('qfcp,cd->qfpd', latents, embed_weight, precision=highest) + token_pos
    normed = stored(modulate(hidden, table, 0, 1))
    queries, keys, values = project_heads(normed, spatial_in, norm_gains, 0)
    mixed = lax.map(spatial_frame, (queries, keys, values))
    branch = jnp.dot(mixed.reshape(-1, HEADS * HD), spatial_out, preferred_element_type=jnp.float32)
    hidden = hidden + table[:, 2][:, None, None, :] * branch.reshape(hidden.shape) + frame_pos
    normed = stored(modulate(hidden, table, 3, 4))
    queries, keys, values = project_heads(normed, temporal_in, norm_gains, 2)
    mixed = temporal_mix(queries, keys, values)
    branch = jnp.dot(mixed.reshape(-1, HEADS * HD), temporal_out, preferred_element_type=jnp.float32)
    hidden = hidden + table[:, 5][:, None, None, :] * branch.reshape(hidden.shape)
    final = modulate(hidden, table, 6, 7)
    return jnp.einsum('qfpd,dc->qfcp', final, final_weight, precision=highest)

def reference(queue_latents, fresh_noise, slot_levels, level_table, embed_weight, spatial_in, spatial_out, temporal_in, temporal_out, norm_gains, final_weight):
    times = (slot_levels.astype(jnp.float32) + 1.0) / LEVELS
    before = jnp.concatenate([jnp.zeros((1,), jnp.float32), times[:-1]])
    stride = times - before
    table = level_table[slot_levels]
    token_pos = sincos(jnp.arange(SPACE_TOK), D)
    frame_pos = sincos(jnp.arange(QUEUE * FRAMES), D).reshape(QUEUE, FRAMES, 1, D)
    latents = queue_latents
    denoised = latents
    for step in range(STEPS):
        velocity = denoise(latents, table, token_pos, frame_pos, embed_weight, spatial_in, spatial_out, temporal_in, temporal_out, norm_gains, final_weight)
        denoised = latents - times[:, None, None, None] * velocity
        moved = latents - stride[:, None, None, None] * velocity
        latents = jnp.concatenate([moved[1:], fresh_noise[step][None]], axis=0)
    return (latents, denoised)
```

```python
import functools
import math

import jax
import jax.numpy as jnp
import numpy as np
from jax import lax
from jax.experimental import pallas as pl
from jax.experimental.pallas import tpu as pltpu
from jax.sharding import PartitionSpec as P

LEVELS = 16
LANES = 128
epsilon = 1e-06
highest = lax.Precision.HIGHEST
f32 = jnp.float32
bf16 = jnp.bfloat16


def sincos(count, width):
    half = width // 2
    rates = np.exp(-np.log(np.float32(10000.0)) * np.arange(half, dtype=np.float32) / np.float32(half))
    angles = np.arange(count, dtype=np.float32)[:, None] * rates[None, :].astype(np.float32)
    return np.concatenate([np.sin(angles), np.cos(angles)], axis=-1).astype(np.float32)


def layer_norm(values):
    centered = values - jnp.mean(values, axis=-1, keepdims=True)
    return centered * lax.rsqrt(jnp.mean(centered * centered, axis=-1, keepdims=True) + epsilon)


def head_norm(values, gain):
    return (
        values * lax.rsqrt(jnp.mean(values * values, axis=-1, keepdims=True) + epsilon) * gain
    ).astype(bf16)


def attention(projected, heads, size, query_gain, key_gain, mask):
    inner = heads * size
    mixed = []
    for head in range(heads):
        at = head * size
        queries = head_norm(projected[:, at : at + size], query_gain)
        keys = head_norm(projected[:, inner + at : inner + at + size], key_gain)
        values = projected[:, 2 * inner + at : 2 * inner + at + size].astype(bf16)
        scores = lax.dot_general(
            queries, keys, (((1,), (1,)), ((), ())), preferred_element_type=f32
        )
        weights = jnp.exp(scores * (1.0 / math.sqrt(size)))
        if mask is not None:
            weights = jnp.where(mask, weights, 0.0)
        totals = jnp.sum(weights, axis=-1, keepdims=True)
        total = jnp.dot(weights.astype(bf16), values, preferred_element_type=f32)
        mixed.append(total / totals)
    return jnp.concatenate(mixed, axis=-1)


def kernel(
    cfg,
    levels,
    start,
    noise,
    level_table,
    pos,
    embed,
    final_weight,
    gains,
    spatial_in_hbm,
    spatial_out_hbm,
    temporal_in_hbm,
    temporal_out_hbm,
    out,
    frame_latents,
    token_latents,
    mix_send,
    mix_recv,
    table,
    hidden,
    normed,
    ends,
    landed,
    spatial_in,
    spatial_out,
    temporal_in,
    temporal_out,
    weight_sem,
    start_send,
    start_recv,
    half_send,
    half_recv,
    mix_send_sem,
    mix_recv_sem,
    lat_send_sem,
    lat_recv_sem,
    end_send,
    end_recv,
):
    sections, shards, repeat = cfg["sections"], cfg["shards"], cfg["repeat"]
    slots, frames, steps = cfg["slots"], cfg["frames"], cfg["steps"]
    heads, size, piece = cfg["heads"], cfg["size"], cfg["piece"]
    width = embed.shape[1]
    group = sections * shards
    own_frames = slots * frames // sections
    rows = slots * frames * piece
    slab = frames * piece
    tokens = group * piece
    section, shard = lax.axis_index("tm"), lax.axis_index("space")
    item = section * shards + shard
    block = shard * sections + section
    frame = item // repeat
    own_slot = frame // frames

    weight_copies = [
        pltpu.make_async_copy(src, dst, weight_sem.at[n])
        for n, (src, dst) in enumerate(
            (
                (spatial_in_hbm, spatial_in),
                (spatial_out_hbm, spatial_out),
                (temporal_in_hbm, temporal_in),
                (temporal_out_hbm, temporal_out),
            )
        )
    ]
    for copy in weight_copies:
        copy.start()

    barrier = pltpu.get_barrier_semaphore()

    def greet(n, carry):
        other = lax.rem(item + n, group)
        pl.semaphore_signal(
            barrier,
            inc=1,
            device_id={"tm": other // shards, "space": lax.rem(other, shards)},
            device_id_type=pl.DeviceIdType.MESH,
        )
        return carry

    lax.fori_loop(1, group, greet, 0)
    pl.semaphore_wait(barrier, group - 1)

    def remote(src, dst, send, recv, to_section, to_shard):
        return pltpu.make_async_remote_copy(
            src_ref=src,
            dst_ref=dst,
            send_sem=send,
            recv_sem=recv,
            device_id={"tm": to_section, "space": to_shard},
            device_id_type=pl.DeviceIdType.MESH,
        )

    def start_copy(n):
        other = lax.rem(shard + n, shards)
        return remote(
            start.at[other // repeat],
            frame_latents.at[pl.ds(shard * sections, sections)],
            start_send.at[n],
            start_recv.at[n],
            section,
            other,
        )

    def half_copy(n):
        other = lax.rem(section + n, sections)
        return remote(
            start.at[:, other],
            token_latents.at[pl.ds(section * own_frames, own_frames)],
            half_send.at[n],
            half_recv.at[n],
            other,
            shard,
        )

    def mix_copy(n):
        other = lax.rem(block + n, group)
        return remote(
            mix_send.at[other],
            mix_recv.at[item],
            mix_send_sem.at[n],
            mix_recv_sem.at[n],
            lax.rem(other, sections),
            other // sections,
        )

    def lat_copy(n):
        other = lax.rem(item + n, group)
        return remote(
            token_latents.at[other // repeat],
            frame_latents.at[block],
            lat_send_sem.at[n],
            lat_recv_sem.at[n],
            other // shards,
            lax.rem(other, shards),
        )

    def end_copy(n):
        other = lax.rem(section + n, sections)
        return remote(
            ends.at[:, pl.ds(other * own_frames, own_frames)],
            landed.at[:, section],
            end_send.at[n],
            end_recv.at[n],
            other,
            shard,
        )

    def start_all(make, count):
        def one(n, carry):
            make(n).start()
            return carry

        lax.fori_loop(1, count, one, 0)

    def wait_all(make, count):
        def one(n, carry):
            make(n).wait()
            return carry

        lax.fori_loop(1, count, one, 0)

    start_all(start_copy, shards)
    start_all(half_copy, sections)
    frame_latents[pl.ds(shard * sections, sections)] = start[shard // repeat]
    token_latents[pl.ds(section * own_frames, own_frames)] = start[:, section]
    for slot in range(slots):
        table[slot] = level_table[levels[slot]]
    wait_all(start_copy, shards)
    wait_all(half_copy, sections)
    for copy in weight_copies:
        copy.wait()

    row_token = lax.rem(lax.broadcasted_iota(jnp.int32, (rows, rows), 0), piece)
    column_token = lax.rem(lax.broadcasted_iota(jnp.int32, (rows, rows), 1), piece)
    same_token = row_token == column_token

    def step_body(step, carry):
        whole = jnp.dot(
            frame_latents[...].reshape(tokens, LANES),
            embed[...],
            precision=highest,
            preferred_element_type=f32,
        )
        shift = table[own_slot, 0:1, :]
        scale = 1.0 + table[own_slot, 1:2, :]
        for at in range(0, tokens, slab):
            part = whole[at : at + slab] + pos[at : at + slab, :]
            normed[at : at + slab, :] = (layer_norm(part) * scale + shift).astype(bf16)
        projected = (
            jnp.dot(normed[0:tokens, :], spatial_in[...], preferred_element_type=f32)
            .astype(bf16)
            .astype(f32)
        )
        mixed = attention(
            projected, heads // repeat, size, gains[0:1, :], gains[1:2, :], None
        )
        mix_send[...] = mixed.reshape(group, piece, heads // repeat * size).astype(bf16)
        start_all(mix_copy, group)
        mix_recv[item] = mix_send[block]

        token_pos = pos[pl.ds(pl.multiple_of(block * piece, piece), piece), :]
        base = jnp.dot(
            token_latents[...].reshape(rows, LANES),
            embed[...],
            precision=highest,
            preferred_element_type=f32,
        )
        for n in range(slots * frames):
            hidden[n * piece : (n + 1) * piece, :] = (
                base[n * piece : (n + 1) * piece] + token_pos
            )
        wait_all(mix_copy, group)
        branch = None
        arrived = mix_recv[...].astype(f32).reshape(
            slots * frames, repeat, piece, heads // repeat * size
        )
        part_width = heads // repeat * size
        for n in range(repeat):
            part = jnp.dot(
                arrived[:, n].reshape(rows, part_width).astype(bf16),
                spatial_out[n * part_width : (n + 1) * part_width, :],
                preferred_element_type=f32,
            )
            branch = part if branch is None else branch + part
        for slot in range(slots):
            at = slot * slab
            frame_pos = jnp.concatenate(
                [
                    jnp.broadcast_to(
                        pos[slot * frames + n : slot * frames + n + 1, :], (piece, width)
                    )
                    for n in range(frames)
                ],
                axis=0,
            )
            part = (
                hidden[at : at + slab, :]
                + table[slot, 2:3, :] * branch[at : at + slab]
                + frame_pos
            )
            hidden[at : at + slab, :] = part
            normed[at : at + slab, :] = (
                layer_norm(part) * (1.0 + table[slot, 4:5, :]) + table[slot, 3:4, :]
            ).astype(bf16)
        projected = (
            jnp.dot(normed[0:rows, :], temporal_in[...], preferred_element_type=f32)
            .astype(bf16)
            .astype(f32)
        )
        mixed = attention(projected, heads, size, gains[2:3, :], gains[3:4, :], same_token)
        branch = jnp.dot(mixed.astype(bf16), temporal_out[...], preferred_element_type=f32)
        for slot in range(slots):
            at = slot * slab
            part = hidden[at : at + slab, :] + table[slot, 5:6, :] * branch[at : at + slab]
            hidden[at : at + slab, :] = (
                layer_norm(part) * (1.0 + table[slot, 7:8, :]) + table[slot, 6:7, :]
            )
        velocity = jnp.dot(
            hidden[...], final_weight[...], precision=highest, preferred_element_type=f32
        ).reshape(slots, frames, piece, LANES)
        before = jnp.float32(0.0)
        for slot in range(slots):
            time = (levels[slot].astype(f32) + 1.0) / LEVELS
            old = token_latents[slot * frames : (slot + 1) * frames]
            ends[1, slot * frames : (slot + 1) * frames] = old - time * velocity[slot]
            if slot > 0:
                token_latents[(slot - 1) * frames : slot * frames] = (
                    old - (time - before) * velocity[slot]
                )
            before = time
        token_latents[(slots - 1) * frames : slots * frames] = noise[step, :, section]

        @pl.when(step < steps - 1)
        def _():
            start_all(lat_copy, group)
            frame_latents[block] = token_latents[frame]
            wait_all(lat_copy, group)

        return carry

    lax.fori_loop(0, steps, step_body, 0)
    ends[0] = token_latents[...]
    start_all(end_copy, sections)
    landed[:, section] = ends[:, pl.ds(section * own_frames, own_frames)]
    wait_all(end_copy, sections)
    out[...] = landed[...]


def per_device(
    queue_latents,
    fresh_noise,
    slot_levels,
    level_table,
    embed_weight,
    spatial_in,
    spatial_out,
    temporal_in,
    temporal_out,
    norm_gains,
    final_weight,
):
    blocks, frames, channels, tokens = queue_latents.shape
    steps, slots = fresh_noise.shape[0], slot_levels.shape[0]
    sections, shards = lax.axis_size("tm"), lax.axis_size("space")
    width, size = embed_weight.shape[1], norm_gains.shape[1]
    inner = spatial_out.shape[0]
    heads = inner // size
    group = sections * shards
    repeat = group // (slots * frames)
    piece = tokens // sections
    own_frames = blocks * frames
    assert repeat * slots * frames == group and heads % repeat == 0
    assert piece * sections == tokens and own_frames * sections == slots * frames
    widen = ((0, 0),) * 3 + ((0, LANES - channels),)
    start = jnp.pad(jnp.transpose(queue_latents, (0, 1, 3, 2)), widen).reshape(
        own_frames, sections, piece, LANES
    )
    noise = jnp.pad(jnp.transpose(fresh_noise, (0, 1, 3, 2)), widen).reshape(
        steps, frames, sections, piece, LANES
    )
    embed = jnp.pad(embed_weight, ((0, LANES - channels), (0, 0)))
    final = jnp.pad(final_weight, ((0, 0), (0, LANES - channels)))
    part = inner // repeat
    if repeat > 1:
        which = lax.rem(lax.axis_index("space"), repeat)
        spatial_in = lax.dynamic_index_in_dim(
            spatial_in.reshape(width, 3, repeat, part), which, axis=2, keepdims=False
        ).reshape(width, 3 * part)
    rows = max(slots * frames * piece, group * piece)
    cfg = dict(
        sections=sections,
        shards=shards,
        repeat=repeat,
        slots=slots,
        frames=frames,
        steps=steps,
        heads=heads,
        size=size,
        piece=piece,
    )
    vmem, anywhere = pl.BlockSpec(memory_space=pltpu.VMEM), pl.BlockSpec(memory_space=pl.ANY)
    dma = pltpu.SemaphoreType.DMA
    out = pl.pallas_call(
        functools.partial(kernel, cfg),
        out_shape=jax.ShapeDtypeStruct((2, sections, own_frames, piece, LANES), f32),
        in_specs=[pl.BlockSpec(memory_space=pltpu.SMEM)] + [vmem] * 7 + [anywhere] * 4,
        out_specs=vmem,
        scratch_shapes=[
            pltpu.VMEM((group, piece, LANES), f32),
            pltpu.VMEM((slots * frames, piece, LANES), f32),
            pltpu.VMEM((group, piece, part), bf16),
            pltpu.VMEM((group, piece, part), bf16),
            pltpu.VMEM((slots, level_table.shape[1], width), f32),
            pltpu.VMEM((slots * frames * piece, width), f32),
            pltpu.VMEM((rows, width), bf16),
            pltpu.VMEM((2, slots * frames, piece, LANES), f32),
            pltpu.VMEM((2, sections, own_frames, piece, LANES), f32),
            pltpu.VMEM(spatial_in.shape, bf16),
            pltpu.VMEM(spatial_out.shape, bf16),
            pltpu.VMEM(temporal_in.shape, bf16),
            pltpu.VMEM(temporal_out.shape, bf16),
            dma((4,)),
            dma((shards,)),
            dma((shards,)),
            dma((sections,)),
            dma((sections,)),
            dma((group,)),
            dma((group,)),
            dma((group,)),
            dma((group,)),
            dma((sections,)),
            dma((sections,)),
        ],
        compiler_params=pltpu.CompilerParams(
            collective_id=0, has_side_effects=True, vmem_limit_bytes=60 * 1024 * 1024
        ),
    )(
        slot_levels,
        start,
        noise,
        level_table,
        jnp.asarray(sincos(max(group * piece, slots * frames), width)),
        embed,
        final,
        norm_gains,
        spatial_in,
        spatial_out,
        temporal_in,
        temporal_out,
    )
    ends = jnp.transpose(out[..., :channels], (0, 2, 4, 1, 3)).reshape(
        2, blocks, frames, channels, tokens
    )
    return (ends[0], ends[1])


def solution(mesh):
    own = P(("clip", "tm"), None, None, "space")
    return jax.shard_map(
        per_device,
        mesh=mesh,
        in_specs=(own, P("clip", None, None, "space"), P("clip")) + (P(),) * 8,
        out_specs=(own, own),
        check_vma=False,
    )
```

```python
import functools
import math

import jax
import jax.numpy as jnp
import numpy as np
from jax import lax
from jax.experimental import pallas as pl
from jax.experimental.pallas import tpu as pltpu
from jax.sharding import PartitionSpec as P

LEVELS = 16
epsilon = 1e-06
f32 = jnp.float32
bf16 = jnp.bfloat16


def sincos(count, width):
    half = width // 2
    rates = np.exp(-np.log(np.float32(10000.0)) * np.arange(half, dtype=np.float32) / np.float32(half))
    angles = np.arange(count, dtype=np.float32)[:, None] * rates[None, :].astype(np.float32)
    return np.concatenate([np.sin(angles), np.cos(angles)], axis=-1).astype(np.float32)


def layer_norm(values):
    centered = values - jnp.mean(values, axis=-1, keepdims=True)
    return centered * lax.rsqrt(jnp.mean(centered * centered, axis=-1, keepdims=True) + epsilon)


def head_norm(values, gain):
    return (
        values * lax.rsqrt(jnp.mean(values * values, axis=-1, keepdims=True) + epsilon) * gain
    ).astype(bf16)


def split(values):
    high = values.astype(bf16)
    return high, (values - high.astype(f32)).astype(bf16)


def heads_of(projected, heads, size, query_gain, key_gain):
    inner = heads * size
    result = []
    for head in range(heads):
        at = head * size
        result.append(
            (
                head_norm(projected[:, at : at + size], query_gain),
                head_norm(projected[:, inner + at : inner + at + size], key_gain),
                projected[:, 2 * inner + at : 2 * inner + at + size].astype(bf16),
            )
        )
    return result


def attention(triples, first, count, mask):
    mixed = []
    for queries, keys, values in triples:
        scores = lax.dot_general(
            queries[first : first + count],
            keys,
            (((1,), (1,)), ((), ())),
            preferred_element_type=f32,
        )
        weights = jnp.exp(scores * (1.0 / math.sqrt(values.shape[1])))
        if mask is not None:
            weights = jnp.where(mask, weights, 0.0)
        totals = jnp.sum(weights, axis=-1, keepdims=True)
        total = jnp.dot(weights.astype(bf16), values, preferred_element_type=f32)
        mixed.append(total / totals)
    return jnp.concatenate(mixed, axis=-1)


def nt_dot(left, right):
    return lax.dot_general(left, right, (((1,), (1,)), ((), ())), preferred_element_type=f32)


def kernel(
    cfg,
    levels,
    start,
    noise,
    level_table,
    pos,
    embed,
    final_weight,
    gains,
    spatial_in_hbm,
    spatial_out_hbm,
    temporal_in_hbm,
    temporal_out_hbm,
    out,
    frame_latents,
    token_latents,
    mix_send,
    mix_recv,
    table,
    hidden,
    normed,
    finals,
    embed_halves,
    final_halves,
    ends,
    landed,
    spatial_in,
    spatial_out,
    temporal_in,
    temporal_out,
    weight_sem,
    start_send,
    start_recv,
    half_send,
    half_recv,
    mix_send_sem,
    mix_recv_sem,
    lat_send_sem,
    lat_recv_sem,
    end_send,
    end_recv,
):
    sections, shards, repeat = cfg["sections"], cfg["shards"], cfg["repeat"]
    slots, frames, steps = cfg["slots"], cfg["frames"], cfg["steps"]
    heads, size, piece = cfg["heads"], cfg["size"], cfg["piece"]
    channels, width = embed.shape
    lanes = piece * channels
    group = sections * shards
    own_frames = slots * frames // sections
    rows = slots * frames * piece
    slab = frames * piece
    tokens = group * piece
    section, shard = lax.axis_index("tm"), lax.axis_index("space")
    item = section * shards + shard
    frame = item // repeat
    own_slot = frame // frames

    weight_copies = [
        pltpu.make_async_copy(src, dst, weight_sem.at[n])
        for n, (src, dst) in enumerate(
            (
                (spatial_in_hbm, spatial_in),
                (spatial_out_hbm, spatial_out),
                (temporal_in_hbm, temporal_in),
                (temporal_out_hbm, temporal_out),
            )
        )
    ]
    for copy in weight_copies:
        copy.start()

    barrier = pltpu.get_barrier_semaphore()

    def greet(n, carry):
        other = lax.rem(item + n, group)
        pl.semaphore_signal(
            barrier,
            inc=1,
            device_id={"tm": other // shards, "space": lax.rem(other, shards)},
            device_id_type=pl.DeviceIdType.MESH,
        )
        return carry

    lax.fori_loop(1, group, greet, 0)
    pl.semaphore_wait(barrier, group - 1)

    def remote(src, dst, send, recv, to_section, to_shard):
        return pltpu.make_async_remote_copy(
            src_ref=src,
            dst_ref=dst,
            send_sem=send,
            recv_sem=recv,
            device_id={"tm": to_section, "space": to_shard},
            device_id_type=pl.DeviceIdType.MESH,
        )

    def start_copy(n):
        other = lax.rem(shard + n, shards)
        return remote(
            start.at[other // repeat],
            frame_latents.at[:, shard],
            start_send.at[n],
            start_recv.at[n],
            section,
            other,
        )

    def half_copy(n):
        other = lax.rem(section + n, sections)
        return remote(
            start.at[:, other],
            token_latents.at[pl.ds(section * own_frames, own_frames)],
            half_send.at[n],
            half_recv.at[n],
            other,
            shard,
        )

    def mix_copy(n):
        other = lax.rem(item + n, group)
        return remote(
            mix_send.at[other],
            mix_recv.at[item],
            mix_send_sem.at[n],
            mix_recv_sem.at[n],
            other // shards,
            lax.rem(other, shards),
        )

    def lat_copy(n):
        other = lax.rem(item + n, group)
        return remote(
            token_latents.at[other // repeat],
            frame_latents.at[section, shard],
            lat_send_sem.at[n],
            lat_recv_sem.at[n],
            other // shards,
            lax.rem(other, shards),
        )

    def end_copy(n):
        other = lax.rem(section + n, sections)
        return remote(
            ends.at[:, pl.ds(other * own_frames, own_frames)],
            landed.at[:, section],
            end_send.at[n],
            end_recv.at[n],
            other,
            shard,
        )

    def start_all(make, count):
        def one(n, carry):
            make(n).start()
            return carry

        lax.fori_loop(1, count, one, 0)

    def wait_all(make, count):
        def one(n, carry):
            make(n).wait()
            return carry

        lax.fori_loop(1, count, one, 0)

    start_all(start_copy, shards)
    start_all(half_copy, sections)
    frame_latents[:, shard] = start[shard // repeat]
    token_latents[pl.ds(section * own_frames, own_frames)] = start[:, section]
    for slot in range(slots):
        table[slot] = level_table[levels[slot]]
    wait_all(start_copy, shards)
    wait_all(half_copy, sections)
    weight_copies[0].wait()

    row_token = lax.rem(lax.broadcasted_iota(jnp.int32, (rows, rows), 0), piece)
    column_token = lax.rem(lax.broadcasted_iota(jnp.int32, (rows, rows), 1), piece)
    same_token = row_token == column_token
    piece_token = lax.broadcasted_iota(jnp.int32, (piece, lanes), 0)
    lane_token = lax.broadcasted_iota(jnp.int32, (piece, lanes), 1) // channels
    own_lanes = piece_token == lane_token
    high, low = split(embed[...])
    embed_halves[...] = jnp.concatenate(
        [high.astype(f32)] * (2 * piece) + [low.astype(f32)] * piece, axis=0
    ).astype(bf16)
    high, low = split(final_weight[...])
    final_halves[...] = jnp.concatenate(
        [high.astype(f32)] * piece + [low.astype(f32)] * piece, axis=0
    ).astype(bf16)

    def embedded(packed):
        spread = jnp.concatenate(
            [jnp.where(own_lanes, jnp.broadcast_to(row, (piece, lanes)), 0.0) for row in packed],
            axis=0,
        )
        high, low = split(spread)
        return jnp.dot(
            jnp.concatenate([high, low, high], axis=1),
            embed_halves[...],
            preferred_element_type=f32,
        )

    def frame_row(n):
        home = n // piece
        return (home % sections * shards + home // sections) * piece + n % piece

    def step_body(step, carry):
        whole = embedded(
            [frame_latents[n // shards, n % shards] for n in range(group)]
        )
        shift = table[own_slot, 0:1, :]
        scale = 1.0 + table[own_slot, 1:2, :]
        for at in range(0, tokens, slab):
            part = whole[at : at + slab] + pos[at : at + slab, :]
            normed[at : at + slab, :] = (layer_norm(part) * scale + shift).astype(bf16)
        projected = nt_dot(normed[0:tokens, :], spatial_in[...]).astype(bf16).astype(f32)
        triples = heads_of(projected, heads // repeat, size, gains[0:1, :], gains[1:2, :])
        part_width = heads // repeat * size
        half = group // 2
        for n in range(2):
            mixed = attention(triples, n * half * piece, half * piece, None)
            mix_send[n * half : (n + 1) * half] = mixed.reshape(half, piece, part_width).astype(
                bf16
            )

            def send(m, carry):
                other = n * half + lax.rem(lax.rem(item, half) + m, half)

                @pl.when(other != item)
                def _():
                    mix_copy(lax.rem(other - item + group, group)).start()

                return carry

            lax.fori_loop(0, half, send, 0)
        mix_recv[item] = mix_send[item]

        token_pos = pos[pl.ds(pl.multiple_of(item * piece, piece), piece), :]
        base = embedded([token_latents[n] for n in range(slots * frames)])
        for n in range(slots * frames):
            hidden[n * piece : (n + 1) * piece, :] = (
                base[n * piece : (n + 1) * piece] + token_pos
            )
        @pl.when(step == 0)
        def _():
            for copy in weight_copies[1:]:
                copy.wait()

        wait_all(mix_copy, group)
        branch = None
        arrived = mix_recv[...].astype(f32).reshape(
            slots * frames, repeat, piece, heads // repeat * size
        )
        for n in range(repeat):
            part = jnp.dot(
                arrived[:, n].reshape(rows, part_width).astype(bf16),
                spatial_out[n * part_width : (n + 1) * part_width, :],
                preferred_element_type=f32,
            )
            branch = part if branch is None else branch + part
        for slot in range(slots):
            at = slot * slab
            frame_pos = jnp.concatenate(
                [
                    jnp.broadcast_to(
                        pos[frame_row(slot * frames + n) : frame_row(slot * frames + n) + 1, :],
                        (piece, width),
                    )
                    for n in range(frames)
                ],
                axis=0,
            )
            part = (
                hidden[at : at + slab, :]
                + table[slot, 2:3, :] * branch[at : at + slab]
                + frame_pos
            )
            hidden[at : at + slab, :] = part
            normed[at : at + slab, :] = (
                layer_norm(part) * (1.0 + table[slot, 4:5, :]) + table[slot, 3:4, :]
            ).astype(bf16)
        projected = nt_dot(normed[0:rows, :], temporal_in[...]).astype(bf16).astype(f32)
        triples = heads_of(projected, heads, size, gains[2:3, :], gains[3:4, :])
        mixed = attention(triples, 0, rows, same_token)
        branch = jnp.dot(mixed.astype(bf16), temporal_out[...], preferred_element_type=f32)
        for slot in range(slots):
            at = slot * slab
            part = hidden[at : at + slab, :] + table[slot, 5:6, :] * branch[at : at + slab]
            final = layer_norm(part) * (1.0 + table[slot, 7:8, :]) + table[slot, 6:7, :]
            high, low = split(final)
            finals[at : at + slab, :] = high
            finals[rows + at : rows + at + slab, :] = low
        product = nt_dot(finals[...], final_halves[...])
        spread = (
            product[0:rows, 0:lanes] + product[0:rows, lanes : 2 * lanes] + product[rows:, 0:lanes]
        )
        for n in range(slots * frames):
            velocity = jnp.sum(
                jnp.where(own_lanes, spread[n * piece : (n + 1) * piece], 0.0),
                axis=0,
                keepdims=True,
            )
            slot = n // frames
            time = (levels[slot].astype(f32) + 1.0) / LEVELS
            before = (levels[slot - 1].astype(f32) + 1.0) / LEVELS if slot > 0 else 0.0
            old = token_latents[n]
            ends[1, n] = old - time * velocity
            if slot > 0:
                token_latents[n - frames] = old - (time - before) * velocity
        for n in range(frames):
            token_latents[(slots - 1) * frames + n] = noise[step, n, section]

        @pl.when(step < steps - 1)
        def _():
            start_all(lat_copy, group)
            frame_latents[section, shard] = token_latents[frame]
            wait_all(lat_copy, group)

        return carry

    lax.fori_loop(0, steps, step_body, 0)
    ends[0] = token_latents[...]
    start_all(end_copy, sections)
    landed[:, section] = ends[:, pl.ds(section * own_frames, own_frames)]
    wait_all(end_copy, sections)
    out[...] = landed[...]


def per_device(
    queue_latents,
    fresh_noise,
    slot_levels,
    level_table,
    embed_weight,
    spatial_in,
    spatial_out,
    temporal_in,
    temporal_out,
    norm_gains,
    final_weight,
):
    blocks, frames, channels, tokens = queue_latents.shape
    steps, slots = fresh_noise.shape[0], slot_levels.shape[0]
    sections, shards = lax.axis_size("tm"), lax.axis_size("space")
    width, size = embed_weight.shape[1], norm_gains.shape[1]
    inner = spatial_out.shape[0]
    heads = inner // size
    group = sections * shards
    repeat = group // (slots * frames)
    piece = tokens // sections
    own_frames = blocks * frames
    assert repeat * slots * frames == group and heads % repeat == 0
    assert piece * sections == tokens and own_frames * sections == slots * frames
    lanes = piece * channels

    def packed(latents):
        return jnp.transpose(latents, (0, 1, 3, 2)).reshape(-1, frames, sections, 1, lanes)

    start = packed(queue_latents).reshape(own_frames, sections, 1, lanes)
    noise = packed(fresh_noise)
    spatial_in, temporal_in, final = spatial_in.T, temporal_in.T, final_weight.T
    part = inner // repeat
    if repeat > 1:
        which = lax.rem(lax.axis_index("space"), repeat)
        spatial_in = lax.dynamic_index_in_dim(
            spatial_in.reshape(3, repeat, part, width), which, axis=1, keepdims=False
        ).reshape(3 * part, width)
    rows = max(slots * frames * piece, group * piece)
    cfg = dict(
        sections=sections,
        shards=shards,
        repeat=repeat,
        slots=slots,
        frames=frames,
        steps=steps,
        heads=heads,
        size=size,
        piece=piece,
    )
    vmem, anywhere = pl.BlockSpec(memory_space=pltpu.VMEM), pl.BlockSpec(memory_space=pl.ANY)
    dma = pltpu.SemaphoreType.DMA
    out = pl.pallas_call(
        functools.partial(kernel, cfg),
        out_shape=jax.ShapeDtypeStruct((2, sections, own_frames, 1, lanes), f32),
        in_specs=[pl.BlockSpec(memory_space=pltpu.SMEM)] + [vmem] * 7 + [anywhere] * 4,
        out_specs=vmem,
        scratch_shapes=[
            pltpu.VMEM((sections, shards, 1, lanes), f32),
            pltpu.VMEM((slots * frames, 1, lanes), f32),
            pltpu.VMEM((group, piece, part), bf16),
            pltpu.VMEM((group, piece, part), bf16),
            pltpu.VMEM((slots, level_table.shape[1], width), f32),
            pltpu.VMEM((slots * frames * piece, width), f32),
            pltpu.VMEM((rows, width), bf16),
            pltpu.VMEM((2 * slots * frames * piece, width), bf16),
            pltpu.VMEM((3 * lanes, width), bf16),
            pltpu.VMEM((2 * lanes, width), bf16),
            pltpu.VMEM((2, slots * frames, 1, lanes), f32),
            pltpu.VMEM((2, sections, own_frames, 1, lanes), f32),
            pltpu.VMEM(spatial_in.shape, bf16),
            pltpu.VMEM(spatial_out.shape, bf16),
            pltpu.VMEM(temporal_in.shape, bf16),
            pltpu.VMEM(temporal_out.shape, bf16),
            dma((4,)),
            dma((shards,)),
            dma((shards,)),
            dma((sections,)),
            dma((sections,)),
            dma((group,)),
            dma((group,)),
            dma((group,)),
            dma((group,)),
            dma((sections,)),
            dma((sections,)),
        ],
        compiler_params=pltpu.CompilerParams(
            collective_id=0, has_side_effects=True, vmem_limit_bytes=60 * 1024 * 1024
        ),
    )(
        slot_levels,
        start,
        noise,
        level_table,
        jnp.asarray(
            sincos(group * piece, width)
            .reshape(shards, sections, piece, width)
            .swapaxes(0, 1)
            .reshape(group * piece, width)
        ),
        embed_weight,
        final,
        norm_gains,
        spatial_in,
        spatial_out,
        temporal_in,
        temporal_out,
    )
    ends = jnp.transpose(
        out.reshape(2, sections, own_frames, piece, channels), (0, 2, 4, 1, 3)
    ).reshape(2, blocks, frames, channels, tokens)
    return (ends[0], ends[1])


def solution(mesh):
    own = P(("clip", "tm"), None, None, "space")
    return jax.shard_map(
        per_device,
        mesh=mesh,
        in_specs=(own, P("clip", None, None, "space"), P("clip")) + (P(),) * 8,
        out_specs=(own, own),
        check_vma=False,
    )
```

```python
import functools
import math

import jax
import jax.numpy as jnp
import numpy as np
from jax import lax
from jax.experimental import pallas as pl
from jax.experimental.pallas import tpu as pltpu
from jax.sharding import PartitionSpec as P

LEVELS = 16
epsilon = 1e-06
f32 = jnp.float32
bf16 = jnp.bfloat16


def sincos(count, width):
    half = width // 2
    rates = np.exp(-np.log(np.float32(10000.0)) * np.arange(half, dtype=np.float32) / np.float32(half))
    angles = np.arange(count, dtype=np.float32)[:, None] * rates[None, :].astype(np.float32)
    return np.concatenate([np.sin(angles), np.cos(angles)], axis=-1).astype(np.float32)


def layer_norm(values):
    centered = values - jnp.mean(values, axis=-1, keepdims=True)
    return centered * lax.rsqrt(jnp.mean(centered * centered, axis=-1, keepdims=True) + epsilon)


def split(values):
    high = values.astype(bf16)
    return high, (values - high.astype(f32)).astype(bf16)


def heads_of(projected, heads, size, gain, head_sum, head_spread):
    inner = heads * size
    rows = projected.shape[0]
    both = projected[:, : 2 * inner]
    high, low = split(both * both)
    sums = jnp.dot(
        jnp.concatenate([high, low], axis=0),
        head_sum[: 2 * inner, :],
        preferred_element_type=f32,
    )
    factor = lax.rsqrt((sums[:rows] + sums[rows:]) * (1.0 / size) + epsilon)
    high, low = split(factor)
    factor = jnp.dot(
        jnp.concatenate([high, low], axis=1),
        head_spread[:, : 2 * inner],
        preferred_element_type=f32,
    )
    both = (both * factor * gain).astype(bf16)
    values = projected[:, 2 * inner :].astype(bf16)
    return [
        (
            both[:, at : at + size],
            both[:, inner + at : inner + at + size],
            values[:, at : at + size],
        )
        for at in range(0, inner, size)
    ]


def attention(triples, first, count, mask):
    mixed = []
    for queries, keys, values in triples:
        scores = lax.dot_general(
            queries[first : first + count],
            keys,
            (((1,), (1,)), ((), ())),
            preferred_element_type=f32,
        )
        weights = jnp.exp2(scores * (math.log2(math.e) / math.sqrt(values.shape[1])))
        if mask is not None:
            weights = jnp.where(mask, weights, 0.0)
        totals = jnp.sum(weights, axis=-1, keepdims=True)
        total = jnp.dot(weights.astype(bf16), values, preferred_element_type=f32)
        mixed.append((total / totals).astype(bf16))
    return jnp.concatenate(mixed, axis=-1)


def nt_dot(left, right):
    return lax.dot_general(left, right, (((1,), (1,)), ((), ())), preferred_element_type=f32)


def kernel(
    cfg,
    levels,
    queue_latents,
    fresh_noise,
    embed,
    final_weight,
    gains,
    level_table_hbm,
    pos_hbm,
    spatial_in_hbm,
    spatial_out_hbm,
    temporal_in_hbm,
    temporal_out_hbm,
    next_queue,
    denoised,
    start,
    noise,
    level_table,
    pos,
    gain_rows,
    head_sum,
    head_spread,
    frame_latents,
    token_latents,
    mix_send,
    mix_recv,
    table,
    hidden,
    normed,
    finals,
    embed_halves,
    final_halves,
    ends,
    landed,
    spatial_in,
    spatial_out,
    temporal_in,
    temporal_out,
    weight_sem,
    start_send,
    start_recv,
    half_send,
    half_recv,
    mix_send_sem,
    mix_recv_sem,
    lat_send_sem,
    lat_recv_sem,
    end_send,
    end_recv,
):
    sections, shards, repeat = cfg["sections"], cfg["shards"], cfg["repeat"]
    slots, frames, steps = cfg["slots"], cfg["frames"], cfg["steps"]
    heads, size, piece = cfg["heads"], cfg["size"], cfg["piece"]
    channels, width = embed.shape
    lanes = piece * channels
    group = sections * shards
    own_frames = slots * frames // sections
    rows = slots * frames * piece
    slab = frames * piece
    tokens = group * piece
    section, shard = lax.axis_index("tm"), lax.axis_index("space")
    item = section * shards + shard
    frame = item // repeat
    own_slot = frame // frames

    weight_copies = [
        pltpu.make_async_copy(src, dst, weight_sem.at[n])
        for n, (src, dst) in enumerate(
            (
                (level_table_hbm, level_table),
                (pos_hbm, pos),
                (spatial_in_hbm, spatial_in),
                (spatial_out_hbm, spatial_out),
                (temporal_in_hbm, temporal_in),
                (temporal_out_hbm, temporal_out),
            )
        )
    ]
    for copy in weight_copies:
        copy.start()

    barrier = pltpu.get_barrier_semaphore()

    def greet(n, carry):
        other = lax.rem(item + n, group)
        pl.semaphore_signal(
            barrier,
            inc=1,
            device_id={"tm": other // shards, "space": lax.rem(other, shards)},
            device_id_type=pl.DeviceIdType.MESH,
        )
        return carry

    lax.fori_loop(1, group, greet, 0)

    def packed(latents, count):
        own_tokens = latents.shape[1]
        wide = sections * lanes
        token = lax.broadcasted_iota(jnp.int32, (own_tokens, wide), 0)
        lane = lax.broadcasted_iota(jnp.int32, (own_tokens, wide), 1)
        spread = jnp.dot(
            latents,
            jnp.where(token == lane // channels, 1.0, 0.0),
            precision=lax.Precision.HIGHEST,
            preferred_element_type=f32,
        )
        channel = lax.broadcasted_iota(jnp.int32, (channels, wide), 0)
        own = channel == lax.rem(lax.broadcasted_iota(jnp.int32, (channels, wide), 1), channels)
        return [
            jnp.sum(
                jnp.where(own, spread[n * channels : (n + 1) * channels], 0.0),
                axis=0,
                keepdims=True,
            )
            for n in range(count)
        ]

    own_tokens = sections * piece
    lines = packed(queue_latents[...].reshape(own_frames * channels, own_tokens), own_frames)
    for n, line in enumerate(lines):
        for t in range(sections):
            start[n, t] = line[:, t * lanes : (t + 1) * lanes]
    pl.semaphore_wait(barrier, group - 1)

    def remote(src, dst, send, recv, to_section, to_shard):
        return pltpu.make_async_remote_copy(
            src_ref=src,
            dst_ref=dst,
            send_sem=send,
            recv_sem=recv,
            device_id={"tm": to_section, "space": to_shard},
            device_id_type=pl.DeviceIdType.MESH,
        )

    def start_copy(n):
        other = lax.rem(shard + n, shards)
        return remote(
            start.at[other // repeat],
            frame_latents.at[:, shard],
            start_send.at[n],
            start_recv.at[n],
            section,
            other,
        )

    def half_copy(n):
        other = lax.rem(section + n, sections)
        return remote(
            start.at[:, other],
            token_latents.at[pl.ds(section * own_frames, own_frames)],
            half_send.at[n],
            half_recv.at[n],
            other,
            shard,
        )

    def mix_copy(n):
        other = lax.rem(item + n, group)
        return remote(
            mix_send.at[other],
            mix_recv.at[item],
            mix_send_sem.at[n],
            mix_recv_sem.at[n],
            other // shards,
            lax.rem(other, shards),
        )

    def lat_copy(n):
        other = lax.rem(item + n, group)
        return remote(
            token_latents.at[other // repeat],
            frame_latents.at[section, shard],
            lat_send_sem.at[n],
            lat_recv_sem.at[n],
            other // shards,
            lax.rem(other, shards),
        )

    def end_copy(n):
        other = lax.rem(section + n, sections)
        return remote(
            ends.at[:, pl.ds(other * own_frames, own_frames)],
            landed.at[:, section],
            end_send.at[n],
            end_recv.at[n],
            other,
            shard,
        )

    def start_all(make, count):
        def one(n, carry):
            make(n).start()
            return carry

        lax.fori_loop(1, count, one, 0)

    def wait_all(make, count):
        def one(n, carry):
            make(n).wait()
            return carry

        lax.fori_loop(1, count, one, 0)

    start_all(start_copy, shards)
    start_all(half_copy, sections)
    frame_latents[:, shard] = start[shard // repeat]
    token_latents[pl.ds(section * own_frames, own_frames)] = start[:, section]
    lines = packed(
        fresh_noise[...].reshape(steps * frames * channels, own_tokens), steps * frames
    )
    for n, line in enumerate(lines):
        for t in range(sections):
            noise[n // frames, n % frames, t] = line[:, t * lanes : (t + 1) * lanes]
    all_heads = 2 * heads * size
    head_sum[...] = jnp.where(
        lax.broadcasted_iota(jnp.int32, (all_heads, 128), 0) // size
        == lax.broadcasted_iota(jnp.int32, (all_heads, 128), 1),
        1.0,
        0.0,
    ).astype(bf16)
    head_spread[...] = jnp.where(
        lax.rem(lax.broadcasted_iota(jnp.int32, (256, all_heads), 0), 128)
        == lax.broadcasted_iota(jnp.int32, (256, all_heads), 1) // size,
        1.0,
        0.0,
    ).astype(bf16)
    for n, count in enumerate((heads // repeat, heads)):
        gain_rows[n : n + 1, : 2 * count * size] = jnp.concatenate(
            [gains[2 * n : 2 * n + 1, :]] * count + [gains[2 * n + 1 : 2 * n + 2, :]] * count,
            axis=1,
        )

    row_token = lax.rem(lax.broadcasted_iota(jnp.int32, (rows, rows), 0), piece)
    column_token = lax.rem(lax.broadcasted_iota(jnp.int32, (rows, rows), 1), piece)
    same_token = row_token == column_token
    piece_token = lax.broadcasted_iota(jnp.int32, (piece, lanes), 0)
    lane_token = lax.broadcasted_iota(jnp.int32, (piece, lanes), 1) // channels
    own_lanes = piece_token == lane_token
    high, low = split(embed[...])
    embed_halves[...] = jnp.concatenate(
        [high.astype(f32)] * (2 * piece) + [low.astype(f32)] * piece, axis=0
    ).astype(bf16)
    high, low = split(final_weight[...])
    final_halves[...] = jnp.concatenate(
        [high.astype(f32)] * piece + [low.astype(f32)] * piece, axis=0
    ).astype(bf16)

    for copy in weight_copies[:2]:
        copy.wait()
    for slot in range(slots):
        table[slot] = level_table[levels[slot]]
    wait_all(start_copy, shards)
    wait_all(half_copy, sections)
    weight_copies[2].wait()

    def embedded(packed):
        spread = jnp.concatenate(
            [jnp.where(own_lanes, jnp.broadcast_to(row, (piece, lanes)), 0.0) for row in packed],
            axis=0,
        )
        high, low = split(spread)
        return jnp.dot(
            jnp.concatenate([high, low, high], axis=1),
            embed_halves[...],
            preferred_element_type=f32,
        )

    def frame_row(n):
        home = n // piece
        return (home % sections * shards + home // sections) * piece + n % piece

    def step_body(step, carry):
        whole = embedded(
            [frame_latents[n // shards, n % shards] for n in range(group)]
        )
        shift = table[own_slot, 0:1, :]
        scale = 1.0 + table[own_slot, 1:2, :]
        for at in range(0, tokens, slab):
            part = whole[at : at + slab] + pos[at : at + slab, :]
            normed[at : at + slab, :] = (layer_norm(part) * scale + shift).astype(bf16)
        projected = nt_dot(normed[0:tokens, :], spatial_in[...]).astype(bf16).astype(f32)
        part_heads = heads // repeat
        triples = heads_of(
            projected,
            part_heads,
            size,
            gain_rows[0:1, : 2 * part_heads * size],
            head_sum,
            head_spread,
        )
        part_width = part_heads * size
        half = group // 2
        for n in range(2):
            mixed = attention(triples, n * half * piece, half * piece, None)
            mix_send[n * half : (n + 1) * half] = (
                mixed.astype(f32).reshape(half, piece, part_width).astype(bf16)
            )

            def send(m, carry):
                other = n * half + lax.rem(lax.rem(item, half) + m, half)

                @pl.when(other != item)
                def _():
                    mix_copy(lax.rem(other - item + group, group)).start()

                return carry

            lax.fori_loop(0, half, send, 0)
        mix_recv[item] = mix_send[item]

        token_pos = pos[pl.ds(pl.multiple_of(item * piece, piece), piece), :]
        base = embedded([token_latents[n] for n in range(slots * frames)])
        for n in range(slots * frames):
            hidden[n * piece : (n + 1) * piece, :] = (
                base[n * piece : (n + 1) * piece] + token_pos
            )
        @pl.when(step == 0)
        def _():
            for copy in weight_copies[3:]:
                copy.wait()

        wait_all(mix_copy, group)
        branch = None
        arrived = mix_recv[...].astype(f32).reshape(
            slots * frames, repeat, piece, heads // repeat * size
        )
        for n in range(repeat):
            part = jnp.dot(
                arrived[:, n].reshape(rows, part_width).astype(bf16),
                spatial_out[n * part_width : (n + 1) * part_width, :],
                preferred_element_type=f32,
            )
            branch = part if branch is None else branch + part
        for slot in range(slots):
            at = slot * slab
            frame_pos = jnp.concatenate(
                [
                    jnp.broadcast_to(
                        pos[frame_row(slot * frames + n) : frame_row(slot * frames + n) + 1, :],
                        (piece, width),
                    )
                    for n in range(frames)
                ],
                axis=0,
            )
            part = (
                hidden[at : at + slab, :]
                + table[slot, 2:3, :] * branch[at : at + slab]
                + frame_pos
            )
            hidden[at : at + slab, :] = part
            normed[at : at + slab, :] = (
                layer_norm(part) * (1.0 + table[slot, 4:5, :]) + table[slot, 3:4, :]
            ).astype(bf16)
        projected = nt_dot(normed[0:rows, :], temporal_in[...]).astype(bf16).astype(f32)
        triples = heads_of(projected, heads, size, gain_rows[1:2, :], head_sum, head_spread)
        mixed = attention(triples, 0, rows, same_token)
        branch = jnp.dot(mixed, temporal_out[...], preferred_element_type=f32)
        for slot in range(slots):
            at = slot * slab
            part = hidden[at : at + slab, :] + table[slot, 5:6, :] * branch[at : at + slab]
            final = layer_norm(part) * (1.0 + table[slot, 7:8, :]) + table[slot, 6:7, :]
            high, low = split(final)
            finals[at : at + slab, :] = high
            finals[rows + at : rows + at + slab, :] = low
        product = nt_dot(finals[...], final_halves[...])
        spread = (
            product[0:rows, 0:lanes] + product[0:rows, lanes : 2 * lanes] + product[rows:, 0:lanes]
        )
        for n in range(slots * frames):
            velocity = jnp.sum(
                jnp.where(own_lanes, spread[n * piece : (n + 1) * piece], 0.0),
                axis=0,
                keepdims=True,
            )
            slot = n // frames
            time = (levels[slot].astype(f32) + 1.0) / LEVELS
            before = (levels[slot - 1].astype(f32) + 1.0) / LEVELS if slot > 0 else 0.0
            old = token_latents[n]
            ends[1, n] = old - time * velocity
            if slot > 0:
                token_latents[n - frames] = old - (time - before) * velocity
        for n in range(frames):
            token_latents[(slots - 1) * frames + n] = noise[step, n, section]

        @pl.when(step < steps - 1)
        def _():
            start_all(lat_copy, group)
            frame_latents[section, shard] = token_latents[frame]
            wait_all(lat_copy, group)

        return carry

    lax.fori_loop(0, steps, step_body, 0)
    ends[0] = token_latents[...]
    start_all(end_copy, sections)
    landed[:, section] = ends[:, pl.ds(section * own_frames, own_frames)]
    wait_all(end_copy, sections)
    spread = jnp.concatenate(
        [
            jnp.where(own_lanes, jnp.broadcast_to(landed[k, t, n], (piece, lanes)), 0.0)
            for k in range(2)
            for n in range(own_frames)
            for t in range(sections)
        ],
        axis=0,
    )
    pick = jnp.where(
        lax.broadcasted_iota(jnp.int32, (channels, lanes), 0)
        == lax.rem(lax.broadcasted_iota(jnp.int32, (channels, lanes), 1), channels),
        1.0,
        0.0,
    )
    result = lax.dot_general(
        pick,
        spread,
        (((1,), (1,)), ((), ())),
        precision=lax.Precision.HIGHEST,
        preferred_element_type=f32,
    )
    for k, target in enumerate((next_queue, denoised)):
        for n in range(own_frames):
            at = (k * own_frames + n) * own_tokens
            target[n // frames, n % frames] = result[:, at : at + own_tokens]


def per_device(
    queue_latents,
    fresh_noise,
    slot_levels,
    level_table,
    embed_weight,
    spatial_in,
    spatial_out,
    temporal_in,
    temporal_out,
    norm_gains,
    final_weight,
):
    blocks, frames, channels, tokens = queue_latents.shape
    steps, slots = fresh_noise.shape[0], slot_levels.shape[0]
    sections, shards = lax.axis_size("tm"), lax.axis_size("space")
    width, size = embed_weight.shape[1], norm_gains.shape[1]
    inner = spatial_out.shape[0]
    heads = inner // size
    group = sections * shards
    repeat = group // (slots * frames)
    piece = tokens // sections
    own_frames = blocks * frames
    assert repeat * slots * frames == group and heads % repeat == 0
    assert piece * sections == tokens and own_frames * sections == slots * frames
    lanes = piece * channels
    spatial_in, temporal_in, final = spatial_in.T, temporal_in.T, final_weight.T
    part = inner // repeat
    if repeat > 1:
        which = lax.rem(lax.axis_index("space"), repeat)
        spatial_in = lax.dynamic_index_in_dim(
            spatial_in.reshape(3, repeat, part, width), which, axis=1, keepdims=False
        ).reshape(3 * part, width)
    rows = max(slots * frames * piece, group * piece)
    cfg = dict(
        sections=sections,
        shards=shards,
        repeat=repeat,
        slots=slots,
        frames=frames,
        steps=steps,
        heads=heads,
        size=size,
        piece=piece,
    )
    vmem, anywhere = pl.BlockSpec(memory_space=pltpu.VMEM), pl.BlockSpec(memory_space=pl.ANY)
    dma = pltpu.SemaphoreType.DMA
    out = pl.pallas_call(
        functools.partial(kernel, cfg),
        out_shape=(jax.ShapeDtypeStruct(queue_latents.shape, f32),) * 2,
        in_specs=[pl.BlockSpec(memory_space=pltpu.SMEM)] + [vmem] * 5 + [anywhere] * 6,
        out_specs=(vmem, vmem),
        scratch_shapes=[
            pltpu.VMEM((own_frames, sections, 1, lanes), f32),
            pltpu.VMEM((steps, frames, sections, 1, lanes), f32),
            pltpu.VMEM(level_table.shape, f32),
            pltpu.VMEM((group * piece, width), f32),
            pltpu.VMEM((2, 2 * inner), f32),
            pltpu.VMEM((2 * inner, 128), bf16),
            pltpu.VMEM((256, 2 * inner), bf16),
            pltpu.VMEM((sections, shards, 1, lanes), f32),
            pltpu.VMEM((slots * frames, 1, lanes), f32),
            pltpu.VMEM((group, piece, part), bf16),
            pltpu.VMEM((group, piece, part), bf16),
            pltpu.VMEM((slots, level_table.shape[1], width), f32),
            pltpu.VMEM((slots * frames * piece, width), f32),
            pltpu.VMEM((rows, width), bf16),
            pltpu.VMEM((2 * slots * frames * piece, width), bf16),
            pltpu.VMEM((3 * lanes, width), bf16),
            pltpu.VMEM((2 * lanes, width), bf16),
            pltpu.VMEM((2, slots * frames, 1, lanes), f32),
            pltpu.VMEM((2, sections, own_frames, 1, lanes), f32),
            pltpu.VMEM(spatial_in.shape, bf16),
            pltpu.VMEM(spatial_out.shape, bf16),
            pltpu.VMEM(temporal_in.shape, bf16),
            pltpu.VMEM(temporal_out.shape, bf16),
            dma((6,)),
            dma((shards,)),
            dma((shards,)),
            dma((sections,)),
            dma((sections,)),
            dma((group,)),
            dma((group,)),
            dma((group,)),
            dma((group,)),
            dma((sections,)),
            dma((sections,)),
        ],
        compiler_params=pltpu.CompilerParams(
            collective_id=0, has_side_effects=True, vmem_limit_bytes=60 * 1024 * 1024
        ),
    )(
        slot_levels,
        queue_latents,
        fresh_noise,
        embed_weight,
        final,
        norm_gains,
        level_table,
        jnp.asarray(
            sincos(group * piece, width)
            .reshape(shards, sections, piece, width)
            .swapaxes(0, 1)
            .reshape(group * piece, width)
        ),
        spatial_in,
        spatial_out,
        temporal_in,
        temporal_out,
    )
    return out


def solution(mesh):
    own = P(("clip", "tm"), None, None, "space")
    return jax.shard_map(
        per_device,
        mesh=mesh,
        in_specs=(own, P("clip", None, None, "space"), P("clip")) + (P(),) * 8,
        out_specs=(own, own),
        check_vma=False,
    )
```

```python
import functools
import math

import jax
import jax.numpy as jnp
import numpy as np
from jax import lax
from jax.experimental import pallas as pl
from jax.experimental.pallas import tpu as pltpu
from jax.sharding import PartitionSpec as P

LEVELS = 16
epsilon = 1e-06
f32 = jnp.float32
bf16 = jnp.bfloat16


def sincos(count, width):
    half = width // 2
    rates = np.exp(-np.log(np.float32(10000.0)) * np.arange(half, dtype=np.float32) / np.float32(half))
    angles = np.arange(count, dtype=np.float32)[:, None] * rates[None, :].astype(np.float32)
    return np.concatenate([np.sin(angles), np.cos(angles)], axis=-1).astype(np.float32)


def layer_norm(values):
    centered = values - jnp.mean(values, axis=-1, keepdims=True)
    return centered * lax.rsqrt(jnp.mean(centered * centered, axis=-1, keepdims=True) + epsilon)


def split(values):
    high = values.astype(bf16)
    return high, (values - high.astype(f32)).astype(bf16)


def heads_of(projected, heads, size, gain, head_sum, head_spread):
    inner = heads * size
    rows = projected.shape[0]
    both = projected[:, : 2 * inner]
    high, low = split(both * both)
    sums = jnp.dot(
        jnp.concatenate([high, low], axis=0),
        head_sum[: 2 * inner, :],
        preferred_element_type=f32,
    )
    factor = lax.rsqrt((sums[:rows] + sums[rows:]) * (1.0 / size) + epsilon)
    high, low = split(factor)
    factor = jnp.dot(
        jnp.concatenate([high, low], axis=1),
        head_spread[:, : 2 * inner],
        preferred_element_type=f32,
    )
    both = (both * factor * gain).astype(bf16)
    values = projected[:, 2 * inner :].astype(bf16)
    return [
        (
            both[:, at : at + size],
            both[:, inner + at : inner + at + size],
            values[:, at : at + size],
        )
        for at in range(0, inner, size)
    ]


def attention(triples, first, count, mask):
    mixed = []
    for queries, keys, values in triples:
        scores = lax.dot_general(
            queries[first : first + count],
            keys,
            (((1,), (1,)), ((), ())),
            preferred_element_type=f32,
        )
        weights = jnp.exp2(scores * (math.log2(math.e) / math.sqrt(values.shape[1])))
        if mask is not None:
            weights = jnp.where(mask, weights, 0.0)
        totals = jnp.sum(weights, axis=-1, keepdims=True)
        total = jnp.dot(weights.astype(bf16), values, preferred_element_type=f32)
        mixed.append((total / totals).astype(bf16))
    return jnp.concatenate(mixed, axis=-1)


def nt_dot(left, right):
    return lax.dot_general(left, right, (((1,), (1,)), ((), ())), preferred_element_type=f32)


def kernel(
    cfg,
    levels,
    queue_latents,
    fresh_noise,
    embed,
    final_weight,
    gains,
    level_table_hbm,
    pos_hbm,
    spatial_in_hbm,
    spatial_out_hbm,
    temporal_in_hbm,
    temporal_out_hbm,
    out,
    start,
    noise,
    level_table,
    pos,
    gain_rows,
    head_sum,
    head_spread,
    frame_latents,
    token_latents,
    mix_send,
    mix_recv,
    table,
    hidden,
    normed,
    finals,
    embed_halves,
    final_halves,
    ends,
    landed,
    spatial_in,
    spatial_out,
    temporal_in,
    temporal_out,
    weight_sem,
    start_send,
    start_recv,
    half_send,
    half_recv,
    mix_send_sem,
    mix_recv_sem,
    lat_send_sem,
    lat_recv_sem,
    end_send,
    end_recv,
):
    sections, shards, repeat = cfg["sections"], cfg["shards"], cfg["repeat"]
    slots, frames, steps = cfg["slots"], cfg["frames"], cfg["steps"]
    heads, size, piece = cfg["heads"], cfg["size"], cfg["piece"]
    channels, width = embed.shape
    lanes = piece * channels
    group = sections * shards
    own_frames = slots * frames // sections
    rows = slots * frames * piece
    slab = frames * piece
    tokens = group * piece
    section, shard = lax.axis_index("tm"), lax.axis_index("space")
    item = section * shards + shard
    frame = item // repeat
    own_slot = frame // frames

    weight_copies = [
        pltpu.make_async_copy(src, dst, weight_sem.at[n])
        for n, (src, dst) in enumerate(
            (
                (level_table_hbm, level_table),
                (pos_hbm, pos),
                (spatial_in_hbm, spatial_in),
                (spatial_out_hbm, spatial_out),
                (temporal_in_hbm, temporal_in),
                (temporal_out_hbm, temporal_out),
            )
        )
    ]
    for copy in weight_copies:
        copy.start()

    barrier = pltpu.get_barrier_semaphore()

    def greet(n, carry):
        other = lax.rem(item + n, group)
        pl.semaphore_signal(
            barrier,
            inc=1,
            device_id={"tm": other // shards, "space": lax.rem(other, shards)},
            device_id_type=pl.DeviceIdType.MESH,
        )
        return carry

    lax.fori_loop(1, group, greet, 0)

    def packed(latents, count):
        own_tokens = latents.shape[1]
        wide = sections * lanes
        token = lax.broadcasted_iota(jnp.int32, (own_tokens, wide), 0)
        lane = lax.broadcasted_iota(jnp.int32, (own_tokens, wide), 1)
        spread = jnp.dot(
            latents,
            jnp.where(token == lane // channels, 1.0, 0.0),
            precision=lax.Precision.HIGHEST,
            preferred_element_type=f32,
        )
        channel = lax.broadcasted_iota(jnp.int32, (channels, wide), 0)
        own = channel == lax.rem(lax.broadcasted_iota(jnp.int32, (channels, wide), 1), channels)
        return [
            jnp.sum(
                jnp.where(own, spread[n * channels : (n + 1) * channels], 0.0),
                axis=0,
                keepdims=True,
            )
            for n in range(count)
        ]

    own_tokens = sections * piece
    lines = packed(queue_latents[...].reshape(own_frames * channels, own_tokens), own_frames)
    for n, line in enumerate(lines):
        for t in range(sections):
            start[n, t] = line[:, t * lanes : (t + 1) * lanes]
    pl.semaphore_wait(barrier, group - 1)

    def remote(src, dst, send, recv, to_section, to_shard):
        return pltpu.make_async_remote_copy(
            src_ref=src,
            dst_ref=dst,
            send_sem=send,
            recv_sem=recv,
            device_id={"tm": to_section, "space": to_shard},
            device_id_type=pl.DeviceIdType.MESH,
        )

    def start_copy(n):
        other = lax.rem(shard + n, shards)
        return remote(
            start.at[other // repeat],
            frame_latents.at[:, shard],
            start_send.at[n],
            start_recv.at[n],
            section,
            other,
        )

    def half_copy(n):
        other = lax.rem(section + n, sections)
        return remote(
            start.at[:, other],
            token_latents.at[pl.ds(section * own_frames, own_frames)],
            half_send.at[n],
            half_recv.at[n],
            other,
            shard,
        )

    def mix_copy(n):
        other = lax.rem(item + n, group)
        return remote(
            mix_send.at[other],
            mix_recv.at[item],
            mix_send_sem.at[n],
            mix_recv_sem.at[n],
            other // shards,
            lax.rem(other, shards),
        )

    def lat_copy(n):
        other = lax.rem(item + n, group)
        return remote(
            token_latents.at[other // repeat],
            frame_latents.at[section, shard],
            lat_send_sem.at[n],
            lat_recv_sem.at[n],
            other // shards,
            lax.rem(other, shards),
        )

    def end_copy(n):
        other = lax.rem(section + n, sections)
        return remote(
            ends.at[:, pl.ds(other * own_frames, own_frames)],
            landed.at[:, section],
            end_send.at[n],
            end_recv.at[n],
            other,
            shard,
        )

    def start_all(make, count):
        def one(n, carry):
            make(n).start()
            return carry

        lax.fori_loop(1, count, one, 0)

    def wait_all(make, count):
        def one(n, carry):
            make(n).wait()
            return carry

        lax.fori_loop(1, count, one, 0)

    start_all(start_copy, shards)
    start_all(half_copy, sections)
    frame_latents[:, shard] = start[shard // repeat]
    token_latents[pl.ds(section * own_frames, own_frames)] = start[:, section]
    lines = packed(
        fresh_noise[...].reshape(steps * frames * channels, own_tokens), steps * frames
    )
    for n, line in enumerate(lines):
        for t in range(sections):
            noise[n // frames, n % frames, t] = line[:, t * lanes : (t + 1) * lanes]
    all_heads = 2 * heads * size
    head_sum[...] = jnp.where(
        lax.broadcasted_iota(jnp.int32, (all_heads, 128), 0) // size
        == lax.broadcasted_iota(jnp.int32, (all_heads, 128), 1),
        1.0,
        0.0,
    ).astype(bf16)
    head_spread[...] = jnp.where(
        lax.rem(lax.broadcasted_iota(jnp.int32, (256, all_heads), 0), 128)
        == lax.broadcasted_iota(jnp.int32, (256, all_heads), 1) // size,
        1.0,
        0.0,
    ).astype(bf16)
    for n, count in enumerate((heads // repeat, heads)):
        gain_rows[n : n + 1, : 2 * count * size] = jnp.concatenate(
            [gains[2 * n : 2 * n + 1, :]] * count + [gains[2 * n + 1 : 2 * n + 2, :]] * count,
            axis=1,
        )

    row_token = lax.rem(lax.broadcasted_iota(jnp.int32, (rows, rows), 0), piece)
    column_token = lax.rem(lax.broadcasted_iota(jnp.int32, (rows, rows), 1), piece)
    same_token = row_token == column_token
    piece_token = lax.broadcasted_iota(jnp.int32, (piece, lanes), 0)
    lane_token = lax.broadcasted_iota(jnp.int32, (piece, lanes), 1) // channels
    own_lanes = piece_token == lane_token
    high, low = split(embed[...])
    embed_halves[...] = jnp.concatenate(
        [high.astype(f32)] * (2 * piece) + [low.astype(f32)] * piece, axis=0
    ).astype(bf16)
    high, low = split(final_weight[...])
    final_halves[...] = jnp.concatenate(
        [high.astype(f32)] * piece + [low.astype(f32)] * piece, axis=0
    ).astype(bf16)

    for copy in weight_copies[:2]:
        copy.wait()
    for slot in range(slots):
        table[slot] = level_table[levels[slot]]
    wait_all(start_copy, shards)
    wait_all(half_copy, sections)
    weight_copies[2].wait()

    def embedded(packed):
        spread = jnp.concatenate(
            [jnp.where(own_lanes, jnp.broadcast_to(row, (piece, lanes)), 0.0) for row in packed],
            axis=0,
        )
        high, low = split(spread)
        return jnp.dot(
            jnp.concatenate([high, low, high], axis=1),
            embed_halves[...],
            preferred_element_type=f32,
        )

    def frame_row(n):
        home = n // piece
        return (home % sections * shards + home // sections) * piece + n % piece

    def step_body(step, carry):
        whole = embedded(
            [frame_latents[n // shards, n % shards] for n in range(group)]
        )
        shift = table[own_slot, 0:1, :]
        scale = 1.0 + table[own_slot, 1:2, :]
        for at in range(0, tokens, slab):
            part = whole[at : at + slab] + pos[at : at + slab, :]
            normed[at : at + slab, :] = (layer_norm(part) * scale + shift).astype(bf16)
        projected = nt_dot(normed[0:tokens, :], spatial_in[...]).astype(bf16).astype(f32)
        part_heads = heads // repeat
        triples = heads_of(
            projected,
            part_heads,
            size,
            gain_rows[0:1, : 2 * part_heads * size],
            head_sum,
            head_spread,
        )
        part_width = part_heads * size
        half = group // 2
        for n in range(2):
            mixed = attention(triples, n * half * piece, half * piece, None)
            mix_send[n * half : (n + 1) * half] = (
                mixed.astype(f32).reshape(half, piece, part_width).astype(bf16)
            )

            def send(m, carry):
                other = n * half + lax.rem(lax.rem(item, half) + m, half)

                @pl.when(other != item)
                def _():
                    mix_copy(lax.rem(other - item + group, group)).start()

                return carry

            lax.fori_loop(0, half, send, 0)
        mix_recv[item] = mix_send[item]

        token_pos = pos[pl.ds(pl.multiple_of(item * piece, piece), piece), :]
        base = embedded([token_latents[n] for n in range(slots * frames)])
        for n in range(slots * frames):
            hidden[n * piece : (n + 1) * piece, :] = (
                base[n * piece : (n + 1) * piece] + token_pos
            )
        @pl.when(step == 0)
        def _():
            for copy in weight_copies[3:]:
                copy.wait()

        wait_all(mix_copy, group)
        branch = None
        arrived = mix_recv[...].astype(f32).reshape(
            slots * frames, repeat, piece, heads // repeat * size
        )
        for n in range(repeat):
            part = jnp.dot(
                arrived[:, n].reshape(rows, part_width).astype(bf16),
                spatial_out[n * part_width : (n + 1) * part_width, :],
                preferred_element_type=f32,
            )
            branch = part if branch is None else branch + part
        for slot in range(slots):
            at = slot * slab
            frame_pos = jnp.concatenate(
                [
                    jnp.broadcast_to(
                        pos[frame_row(slot * frames + n) : frame_row(slot * frames + n) + 1, :],
                        (piece, width),
                    )
                    for n in range(frames)
                ],
                axis=0,
            )
            part = (
                hidden[at : at + slab, :]
                + table[slot, 2:3, :] * branch[at : at + slab]
                + frame_pos
            )
            hidden[at : at + slab, :] = part
            normed[at : at + slab, :] = (
                layer_norm(part) * (1.0 + table[slot, 4:5, :]) + table[slot, 3:4, :]
            ).astype(bf16)
        projected = nt_dot(normed[0:rows, :], temporal_in[...]).astype(bf16).astype(f32)
        triples = heads_of(projected, heads, size, gain_rows[1:2, :], head_sum, head_spread)
        mixed = attention(triples, 0, rows, same_token)
        branch = jnp.dot(mixed, temporal_out[...], preferred_element_type=f32)
        for slot in range(slots):
            at = slot * slab
            part = hidden[at : at + slab, :] + table[slot, 5:6, :] * branch[at : at + slab]
            final = layer_norm(part) * (1.0 + table[slot, 7:8, :]) + table[slot, 6:7, :]
            high, low = split(final)
            finals[at : at + slab, :] = high
            finals[rows + at : rows + at + slab, :] = low
        product = nt_dot(finals[...], final_halves[...])
        spread = (
            product[0:rows, 0:lanes] + product[0:rows, lanes : 2 * lanes] + product[rows:, 0:lanes]
        )
        for n in range(slots * frames):
            velocity = jnp.sum(
                jnp.where(own_lanes, spread[n * piece : (n + 1) * piece], 0.0),
                axis=0,
                keepdims=True,
            )
            slot = n // frames
            time = (levels[slot].astype(f32) + 1.0) / LEVELS
            before = (levels[slot - 1].astype(f32) + 1.0) / LEVELS if slot > 0 else 0.0
            old = token_latents[n]
            ends[1, n] = old - time * velocity
            if slot > 0:
                token_latents[n - frames] = old - (time - before) * velocity
        for n in range(frames):
            token_latents[(slots - 1) * frames + n] = noise[step, n, section]

        @pl.when(step < steps - 1)
        def _():
            start_all(lat_copy, group)
            frame_latents[section, shard] = token_latents[frame]
            wait_all(lat_copy, group)

        return carry

    lax.fori_loop(0, steps, step_body, 0)
    ends[0] = token_latents[...]
    start_all(end_copy, sections)
    landed[:, section] = ends[:, pl.ds(section * own_frames, own_frames)]
    wait_all(end_copy, sections)
    out[...] = landed[...]


def unpack(frames, landed, next_queue, denoised):
    _, sections, own_frames, _, lanes = landed.shape
    channels = next_queue.shape[2]
    piece = lanes // channels
    own_tokens = sections * piece
    piece_token = lax.broadcasted_iota(jnp.int32, (piece, lanes), 0)
    own_lanes = piece_token == lax.broadcasted_iota(jnp.int32, (piece, lanes), 1) // channels
    spread = jnp.concatenate(
        [
            jnp.where(own_lanes, jnp.broadcast_to(landed[k, t, n], (piece, lanes)), 0.0)
            for k in range(2)
            for n in range(own_frames)
            for t in range(sections)
        ],
        axis=0,
    )
    pick = jnp.where(
        lax.broadcasted_iota(jnp.int32, (channels, lanes), 0)
        == lax.rem(lax.broadcasted_iota(jnp.int32, (channels, lanes), 1), channels),
        1.0,
        0.0,
    )
    result = lax.dot_general(
        pick,
        spread,
        (((1,), (1,)), ((), ())),
        precision=lax.Precision.HIGHEST,
        preferred_element_type=f32,
    )
    for k, target in enumerate((next_queue, denoised)):
        for n in range(own_frames):
            at = (k * own_frames + n) * own_tokens
            target[n // frames, n % frames] = result[:, at : at + own_tokens]


def per_device(
    queue_latents,
    fresh_noise,
    slot_levels,
    level_table,
    embed_weight,
    spatial_in,
    spatial_out,
    temporal_in,
    temporal_out,
    norm_gains,
    final_weight,
):
    blocks, frames, channels, tokens = queue_latents.shape
    steps, slots = fresh_noise.shape[0], slot_levels.shape[0]
    sections, shards = lax.axis_size("tm"), lax.axis_size("space")
    width, size = embed_weight.shape[1], norm_gains.shape[1]
    inner = spatial_out.shape[0]
    heads = inner // size
    group = sections * shards
    repeat = group // (slots * frames)
    piece = tokens // sections
    own_frames = blocks * frames
    assert repeat * slots * frames == group and heads % repeat == 0
    assert piece * sections == tokens and own_frames * sections == slots * frames
    lanes = piece * channels
    spatial_in, temporal_in, final = spatial_in.T, temporal_in.T, final_weight.T
    part = inner // repeat
    if repeat > 1:
        which = lax.rem(lax.axis_index("space"), repeat)
        spatial_in = lax.dynamic_index_in_dim(
            spatial_in.reshape(3, repeat, part, width), which, axis=1, keepdims=False
        ).reshape(3 * part, width)
    rows = max(slots * frames * piece, group * piece)
    cfg = dict(
        sections=sections,
        shards=shards,
        repeat=repeat,
        slots=slots,
        frames=frames,
        steps=steps,
        heads=heads,
        size=size,
        piece=piece,
    )
    vmem, anywhere = pl.BlockSpec(memory_space=pltpu.VMEM), pl.BlockSpec(memory_space=pl.ANY)
    dma = pltpu.SemaphoreType.DMA
    landed = pl.pallas_call(
        functools.partial(kernel, cfg),
        out_shape=jax.ShapeDtypeStruct((2, sections, own_frames, 1, lanes), f32),
        in_specs=[pl.BlockSpec(memory_space=pltpu.SMEM)] + [vmem] * 5 + [anywhere] * 6,
        out_specs=vmem,
        scratch_shapes=[
            pltpu.VMEM((own_frames, sections, 1, lanes), f32),
            pltpu.VMEM((steps, frames, sections, 1, lanes), f32),
            pltpu.VMEM(level_table.shape, f32),
            pltpu.VMEM((group * piece, width), f32),
            pltpu.VMEM((2, 2 * inner), f32),
            pltpu.VMEM((2 * inner, 128), bf16),
            pltpu.VMEM((256, 2 * inner), bf16),
            pltpu.VMEM((sections, shards, 1, lanes), f32),
            pltpu.VMEM((slots * frames, 1, lanes), f32),
            pltpu.VMEM((group, piece, part), bf16),
            pltpu.VMEM((group, piece, part), bf16),
            pltpu.VMEM((slots, level_table.shape[1], width), f32),
            pltpu.VMEM((slots * frames * piece, width), f32),
            pltpu.VMEM((rows, width), bf16),
            pltpu.VMEM((2 * slots * frames * piece, width), bf16),
            pltpu.VMEM((3 * lanes, width), bf16),
            pltpu.VMEM((2 * lanes, width), bf16),
            pltpu.VMEM((2, slots * frames, 1, lanes), f32),
            pltpu.VMEM((2, sections, own_frames, 1, lanes), f32),
            pltpu.VMEM(spatial_in.shape, bf16),
            pltpu.VMEM(spatial_out.shape, bf16),
            pltpu.VMEM(temporal_in.shape, bf16),
            pltpu.VMEM(temporal_out.shape, bf16),
            dma((6,)),
            dma((shards,)),
            dma((shards,)),
            dma((sections,)),
            dma((sections,)),
            dma((group,)),
            dma((group,)),
            dma((group,)),
            dma((group,)),
            dma((sections,)),
            dma((sections,)),
        ],
        compiler_params=pltpu.CompilerParams(
            collective_id=0, has_side_effects=True, vmem_limit_bytes=60 * 1024 * 1024
        ),
    )(
        slot_levels,
        queue_latents,
        fresh_noise,
        embed_weight,
        final,
        norm_gains,
        level_table,
        jnp.asarray(
            sincos(group * piece, width)
            .reshape(shards, sections, piece, width)
            .swapaxes(0, 1)
            .reshape(group * piece, width)
        ),
        spatial_in,
        spatial_out,
        temporal_in,
        temporal_out,
    )
    return pl.pallas_call(
        functools.partial(unpack, frames),
        out_shape=(jax.ShapeDtypeStruct(queue_latents.shape, f32),) * 2,
        in_specs=[vmem],
        out_specs=(vmem, vmem),
    )(landed)


def solution(mesh):
    own = P(("clip", "tm"), None, None, "space")
    return jax.shard_map(
        per_device,
        mesh=mesh,
        in_specs=(own, P("clip", None, None, "space"), P("clip")) + (P(),) * 8,
        out_specs=(own, own),
        check_vma=False,
    )
```
